32 devices in a mesh: groups: 1, row: 32 (over z, y, x, core).
Axes of the slice: x: 2, y: 2, z: 4, core: 2. Of those that a mesh axis runs over, the one named last changes fastest.
Arguments:
- latents: bfloat16 [2048, 1024], P(('groups', 'row')), may hold values from -6 to 6
- expert_ids: int32 [2048, 22], P(('groups', 'row')), may hold values from 0 to 63, all different within a row; in each aligned block of 64 rows (0 to 63, 64 to 127, ...) at most 33 rows name the same one
- gates: float32 [2048, 22], P(('groups', 'row')), may hold values from 0.02 to 0.2
- w_up: bfloat16 [64, 1024, 1344], P('row'), may hold values from -0.1875 to 0.1875
- w_down: bfloat16 [64, 1344, 1024], P('row'), may hold values from -0.15625 to 0.15625
Outputs:
- combined: bfloat16 [2048, 1024], P(('groups', 'row'))
The draws below stay inside these ranges and needn't reach their ends.
Inputs may be any that keep to these rules, and one draw needn't show every extreme that they name: `expert_ids`: in each aligned block of 64 rows, each expert is named by at most 33 rows, a bound that some block reaches; a row names 22 different experts.
All inputs are finite; a program needn't handle non-finite values.
Results may differ from the reference program's by a relative error of at most 0.0058.
Values may be sent and summed in bfloat16 or wider, within the bound.
A program may use at most 64 MiB of HBM per device.

```python
import math
import jax
import jax.numpy as jnp
import numpy as np
from jax import lax

L = 1024
H = 1344
TOP = 22
TOK_DEV = 64
EXPERTS = 64
TOKENS = 2048
CAP = 33
N_ROW = 32


def levels(key, shape, cuts, smallest, largest):
    def one(axis_at, blocks):
        steps = jax.random.uniform(jax.random.fold_in(jax.random.fold_in(key, 6), axis_at), (blocks,), jnp.float32, smallest / len(cuts), largest / len(cuts))
        return jnp.repeat(jnp.exp(steps), shape[axis_at] // blocks).reshape((-1,) + (1,) * (len(shape) - axis_at - 1))

    loudness = one(*cuts[0])
    for cut in cuts[1:]:
        loudness = loudness * one(*cut)
    return loudness


def assign_block(own_key, own, number, rows, number_of, top, limit, skew):
    sequence = jax.random.permutation(own_key, number_of)
    heavy_load, common = shares(number_of, rows * top, limit, skew, True), shares(number_of, rows * top, limit, skew, False)
    places = jnp.arange(number_of)

    def named(tallies, rotation):
        used = int((tallies > 0).sum())
        fixed = max(1, used // 4)
        moved = fixed + (places - fixed + rotation * (used - fixed)) % max(1, number_of - fixed)
        return jnp.zeros((number_of,), jnp.int32).at[sequence[jnp.where(places < fixed, places, moved)]].set(jnp.asarray(tallies, jnp.int32))

    tallies = jnp.where(number % 4 == 0, named(heavy_load, number // 4), named(common, number - number // 4 - 1))
    mixed = jax.random.permutation(jax.random.fold_in(own, 3), number_of)
    donor, sink = mixed[0:number_of // 2 * 2:2], mixed[1:number_of // 2 * 2:2]
    slack = jnp.minimum(tallies[donor] - 1, limit - tallies[sink]) // 2
    slack = jnp.where((donor == sequence[0]) | (sink == sequence[0]) | (tallies[sink] == 0), 0, jnp.maximum(slack, 0))
    moved = jax.random.randint(jax.random.fold_in(own, 4), (number_of // 2,), 0, 1 << 20) % (slack + 1)
    tallies = tallies.at[donor].add(-moved).at[sink].add(moved)
    items = jnp.searchsorted(jnp.cumsum(tallies), jnp.arange(rows * top), side="right").astype(jnp.int32)
    grid = items.reshape(top, rows).T
    grid = grid[jax.random.permutation(jax.random.fold_in(own, 1), rows)]
    rotation = jax.random.randint(jax.random.fold_in(own, 2), (rows, 1), 0, top)
    return jnp.take_along_axis(grid, (jnp.arange(top)[None, :] + rotation) % top, axis=1)


def shares(number_of, total, limit, skew, full):
    loads = [(1 << 20) // math.isqrt(rank ** skew) + 1 for rank in range(1, number_of + 1)]
    largest = limit if full else min(limit, max(-(-total // number_of), total * loads[0] // sum(loads)))
    least = 1 if total - largest >= number_of - 1 else 0
    holding, spare = [largest] + [least] * (number_of - 1), total - largest - least * (number_of - 1)
    while spare > 0:
        candidates = [i for i in range(1, number_of) if holding[i] < largest] or [i for i in range(1, number_of) if holding[i] < limit]
        whole, left = sum([loads[i] for i in candidates]), spare
        for i in candidates:
            addition = min(limit - holding[i], max(1, left * loads[i] // whole), spare)
            holding[i] = holding[i] + addition
            spare = spare - addition
    return np.array(holding)


def bell_draw(rng, extent, width, bound, pieces=(), held_as=jnp.bfloat16):
    entries = jax.random.normal(rng, extent, jnp.float32) * width
    if len(pieces) > 0:
        entries = levels(rng, extent, pieces, -0.22, 0.18) * entries
    return jnp.clip(entries, min=-bound, max=bound).astype(held_as)


def setup_inputs(seed: int = 0, part: int = 0) -> dict:
    streams_of = jax.random.split(jax.random.key(seed), 6)
    part_splits = jax.random.split(jax.random.fold_in(streams_of[5], part), 6)
    latents = bell_draw(part_splits[0], (TOKENS, L), 1.0, 6.0, ((0, 32),))
    expert_ids_keys = jax.random.split(jax.random.fold_in(part_splits[1], 1), TOKENS // TOK_DEV)
    expert_ids_turns = jax.random.permutation(jax.random.fold_in(part_splits[1], 3), TOKENS // TOK_DEV)
    expert_ids = jax.vmap(lambda own, number: assign_block(jax.random.fold_in(part_splits[1], 2), own, number, TOK_DEV, EXPERTS, TOP, CAP, 1))(expert_ids_keys, expert_ids_turns).reshape((TOKENS, TOP))
    gates = jnp.clip(jnp.exp(math.log(0.2) - 2.3025851 * jax.random.uniform(part_splits[2], (TOKENS, TOP), jnp.float32) ** levels(part_splits[2], (TOKENS, TOP), ((0, 32),), -0.2, 0.2)), 0.02, 0.2)
    w_up = bell_draw(streams_of[3], (EXPERTS, L, H), L ** -0.5, 0.1875, ((0, 32),))
    w_down = bell_draw(streams_of[4], (EXPERTS, H, L), H ** -0.5, 0.15625, ((0, 32),))
    return {"latents": latents, "expert_ids": expert_ids, "gates": gates, "w_up": w_up, "w_down": w_down}


def slot_numbers(flat_ids, experts):
    labels = jnp.arange(experts, dtype=jnp.int32)
    onehot = (flat_ids[:, None] == labels[None, :]).astype(jnp.int32)
    before = jnp.cumsum(onehot, axis=0) - onehot
    return jnp.sum(before * onehot, axis=1).astype(jnp.int32)


def reference(latents, expert_ids, gates, w_up, w_down):
    block_ids = expert_ids.reshape(N_ROW, TOK_DEV * TOP).astype(jnp.int32)
    block_slots = lax.map(lambda row_ids: slot_numbers(row_ids, EXPERTS), block_ids)
    sources = jnp.arange(N_ROW, dtype=jnp.int32)[:, None]
    columns = (sources * CAP + block_slots).astype(jnp.int32)
    owners = (sources * TOK_DEV + jnp.arange(TOK_DEV * TOP, dtype=jnp.int32)[None, :] // TOP).astype(jnp.int32)
    lookup = jnp.full((EXPERTS, N_ROW * CAP), TOKENS, jnp.int32).at[block_ids, columns].set(owners)
    weighting = jnp.zeros((EXPERTS, N_ROW * CAP), jnp.float32).at[block_ids, columns].set(gates.reshape(N_ROW, TOK_DEV * TOP))
    padded = jnp.concatenate([latents, jnp.zeros((1, L), latents.dtype)], axis=0)

    def visit(total, inputs):
        row_index, row_gates, up_matrix, down_matrix = inputs
        rows = padded[row_index]
        hidden = jnp.dot(rows, up_matrix, preferred_element_type=jnp.float32)
        active = jnp.square(jnp.maximum(hidden, 0.0)).astype(jnp.bfloat16)
        output = jnp.dot(active, down_matrix, preferred_element_type=jnp.float32).astype(jnp.bfloat16)
        total = total.at[row_index].add(row_gates[:, None] * output.astype(jnp.float32))
        return total, None

    total, unused = lax.scan(visit, jnp.zeros((TOKENS + 1, L), jnp.float32), (lookup, weighting, w_up, w_down))
    return total[:TOKENS].astype(jnp.bfloat16)
```

```python
import functools
import jax
import jax.numpy as jnp
from jax import lax
from jax.experimental import pallas as pl
from jax.experimental.pallas import tpu as pltpu
from jax.sharding import PartitionSpec as P

CORES = 2


def kernel(Z, Q, experts, xin, wu_hbm, wd_hbm, out, X, wu, wd, PP, RP, R, DH, XY, S, ZR, F, sel, sa, ra, sr, rr, wsem):
    T, W = xin.shape
    local_experts, L, H = wu.shape
    G = W - L
    half = T // 2
    layer = CORES * Q
    me = lax.axis_index("row")
    c = lax.rem(me, CORES)
    q = lax.rem(me // CORES, Q)
    z = me // layer
    inner = lax.rem(me, layer)
    partner = me + 1 - 2 * c
    if Q > 1:
        x = lax.rem(q, 2)
        y = q // 2
        xn, yn = me + CORES * (1 - 2 * x), me + 2 * CORES * (1 - 2 * y)
        qx, qy, qd = q + 1 - 2 * x, q + 2 * (1 - 2 * y), 3 - q

    def remote(src, dst, ssem, rsem, dev):
        return pltpu.make_async_remote_copy(
            src_ref=src, dst_ref=dst, send_sem=ssem, recv_sem=rsem,
            device_id={"row": dev}, device_id_type=pl.DeviceIdType.MESH,
        )

    weights = [
        pltpu.make_async_copy(wu_hbm, wu, wsem.at[0]),
        pltpu.make_async_copy(wd_hbm, wd, wsem.at[1]),
    ]
    local = pltpu.make_async_copy(xin, X.at[0, c, q], wsem.at[2])
    local.start()
    for w in weights:
        w.start()

    barrier = pltpu.get_barrier_semaphore()
    near = [partner] + ([xn, yn] if Q > 1 else [])
    for dev in near:
        pl.semaphore_signal(barrier, inc=1, device_id={"row": dev}, device_id_type=pl.DeviceIdType.MESH)

    def below(k):
        return lax.rem(z - k + Z, Z) * layer + inner

    def above(k):
        return lax.rem(z + k, Z) * layer + inner

    def greet(k, carry):
        pl.semaphore_signal(barrier, inc=1, device_id={"row": below(k)}, device_id_type=pl.DeviceIdType.MESH)
        return carry

    lax.fori_loop(1, Z, greet, 0)
    pl.semaphore_wait(barrier, len(near) + Z - 1)

    def zcopy(k):
        return remote(xin, X.at[k, c, q], sa.at[k, 0], ra.at[k, 0], below(k))

    def xcopy(k):
        return remote(X.at[k, c, q], X.at[k, c, q], sa.at[k, 1], ra.at[k, 1], xn)

    def ycopy(k):
        return remote(X.at[k, c, q], X.at[k, c, q], sa.at[k, 2], ra.at[k, 2], yn)

    def top(k, slot):
        ref = X.at[k, c, slot, pl.ds(0, half)]
        return remote(ref, ref, sa.at[k, 3], ra.at[k, 3], yn)

    def bottom(k, slot):
        ref = X.at[k, c, slot, pl.ds(half, half)]
        return remote(ref, ref, sa.at[k, 4], ra.at[k, 4], xn)

    def across(k, slot, i, plane):
        ref = X.at[k, plane, slot]
        return remote(ref, ref, sa.at[k, 5 + i], ra.at[k, 5 + i], partner)

    def arrived(k, ref, i):
        remote(ref, ref, sa.at[k, i], ra.at[k, i], partner).wait_recv()

    def ag_send(k):
        if Q > 1:
            xcopy(k).start()
            ycopy(k).start()
        across(k, q, 0, c).start()

    def ag_relay(k):
        if Q > 1:
            arrived(k, X.at[k, c, qx], 1)
            top(k, qx).start()
            arrived(k, X.at[k, c, qy], 2)
            bottom(k, qy).start()
            across(k, qx, 1, c).start()
            across(k, qy, 2, c).start()

    def ag_last(k):
        if Q > 1:
            arrived(k, X.at[k, c, qd, pl.ds(0, half)], 3)
            arrived(k, X.at[k, c, qd, pl.ds(half, half)], 4)
            across(k, qd, 3, c).start()

    def ag_other(k):
        arrived(k, X.at[k, 1 - c, q], 5)
        if Q > 1:
            arrived(k, X.at[k, 1 - c, qx], 6)
            arrived(k, X.at[k, 1 - c, qy], 7)
            arrived(k, X.at[k, 1 - c, qd], 8)

    def compute(k, plane):
        rows = X[k, plane, :, :, pl.ds(0, L)].reshape(Q * T, L)
        codes = X[k, plane, :, :, pl.ds(L, G)].reshape(Q * T, G)
        weight = jnp.dot(codes, sel[...], preferred_element_type=jnp.float32)
        total = None
        for e in range(local_experts):
            hidden = jnp.dot(rows, wu[e], preferred_element_type=jnp.float32)
            active = jnp.square(jnp.maximum(hidden, 0.0)).astype(jnp.bfloat16)
            part = jnp.dot(active, wd[e], preferred_element_type=jnp.float32)
            part = part * jnp.tile(weight[:, e * 128 : (e + 1) * 128], (1, L // 128))
            total = part if total is None else total + part
        return total

    def swap(k):
        return remote(PP.at[k], RP.at[k], sr.at[k, 0], rr.at[k, 0], partner)

    def dtop(k):
        return remote(R.at[k, qd, pl.ds(0, half)], DH.at[k, 0], sr.at[k, 1], rr.at[k, 1], yn)

    def dbottom(k):
        return remote(R.at[k, qd, pl.ds(half, half)], DH.at[k, 1], sr.at[k, 2], rr.at[k, 2], xn)

    def xsum(k):
        return remote(R.at[k, qx], XY.at[k, 0], sr.at[k, 3], rr.at[k, 3], xn)

    def ysum(k):
        return remote(R.at[k, qy], XY.at[k, 1], sr.at[k, 4], rr.at[k, 4], yn)

    def zsum(k):
        return remote(S.at[k], ZR.at[k], sr.at[k, 5], rr.at[k, 5], above(k))

    def rs_near(k):
        if Q > 1:
            dtop(k).wait_recv()
            R[k, qx, pl.ds(0, half)] = (
                R[k, qx, pl.ds(0, half)].astype(jnp.float32) + DH[k, 0].astype(jnp.float32)
            ).astype(jnp.bfloat16)
            xsum(k).start()
            dbottom(k).wait_recv()
            R[k, qy, pl.ds(half, half)] = (
                R[k, qy, pl.ds(half, half)].astype(jnp.float32) + DH[k, 1].astype(jnp.float32)
            ).astype(jnp.bfloat16)
            ysum(k).start()

    def rs_far(k):
        value = R[k, q].astype(jnp.float32)
        if Q > 1:
            xsum(k).wait_recv()
            value = value + XY[k, 0].astype(jnp.float32)
            ysum(k).wait_recv()
            value = value + XY[k, 1].astype(jnp.float32)

        @pl.when(k == 0)
        def _():
            F[...] = value

        @pl.when(k > 0)
        def _():
            S[k] = value.astype(jnp.bfloat16)
            zsum(k).start()

    local.wait()
    ag_send(0)

    def send_down(k, carry):
        zcopy(k).start()
        return carry

    lax.fori_loop(1, Z, send_down, 0)
    entry = lax.rem(lax.broadcasted_iota(jnp.int32, sel.shape, 0), experts)
    lane = lax.broadcasted_iota(jnp.int32, sel.shape, 1) // 128
    used = lax.broadcasted_iota(jnp.int32, sel.shape, 0) < 2 * experts
    sel[...] = jnp.where((entry == me * local_experts + lane) & used, 1.0, 0.0).astype(jnp.bfloat16)
    ag_relay(0)
    ag_last(0)
    for w in weights:
        w.wait()

    def step(k, carry):
        ag_other(k)

        @pl.when(k + 1 < Z)
        def _():
            arrived(k + 1, X.at[k + 1, c, q], 0)
            ag_send(k + 1)

        PP[k] = compute(k, 1 - c).astype(jnp.bfloat16)
        swap(k).start()

        @pl.when(k > 0)
        def _():
            rs_near(k - 1)

        @pl.when(k + 1 < Z)
        def _():
            ag_relay(k + 1)

        mine = compute(k, c)
        swap(k).wait_recv()
        R[k] = (mine + RP[k].astype(jnp.float32)).astype(jnp.bfloat16).reshape(Q, T, L)
        if Q > 1:
            dtop(k).start()
            dbottom(k).start()

        @pl.when(k + 1 < Z)
        def _():
            ag_last(k + 1)

        @pl.when(k > 0)
        def _():
            rs_far(k - 1)

        return carry

    lax.fori_loop(0, Z, step, 0)
    rs_near(Z - 1)
    rs_far(Z - 1)

    def collect(k, carry):
        zsum(k).wait_recv()
        F[...] += ZR[k].astype(jnp.float32)
        return carry

    lax.fori_loop(1, Z, collect, 0)
    out[...] = F[...].astype(out.dtype)

    def drain(k, carry):
        across(k, q, 0, c).wait_send()
        swap(k).wait_send()
        if Q > 1:
            xcopy(k).wait_send()
            ycopy(k).wait_send()
            top(k, qx).wait_send()
            bottom(k, qy).wait_send()
            across(k, qx, 1, c).wait_send()
            across(k, qy, 2, c).wait_send()
            across(k, qd, 3, c).wait_send()
            dtop(k).wait_send()
            dbottom(k).wait_send()
            xsum(k).wait_send()
            ysum(k).wait_send()

        @pl.when(k > 0)
        def _():
            zcopy(k).wait_send()
            zsum(k).wait_send()

        return carry

    lax.fori_loop(0, Z, drain, 0)


def body(groups, latents, expert_ids, gates, w_up, w_down):
    n = lax.axis_size("row")
    T, L = latents.shape
    local_experts, unused, H = w_up.shape
    experts = n * local_experts
    Q = 4 if groups == 1 and n % (4 * CORES) == 0 else 1
    Z = n // (CORES * Q)
    labels = jnp.arange(experts, dtype=jnp.int32)
    dense = jnp.sum(
        jnp.where(expert_ids[:, :, None] == labels[None, None, :], gates[:, :, None], 0.0), axis=1
    )
    coarse = lax.reduce_precision(dense, 8, 7)
    G = -(-2 * experts // 128) * 128
    pad = jnp.zeros((T, G - 2 * experts), jnp.bfloat16)
    rows = jnp.concatenate(
        [latents, coarse.astype(jnp.bfloat16), (dense - coarse).astype(jnp.bfloat16), pad], axis=1
    )
    bf16 = jnp.bfloat16
    return pl.pallas_call(
        functools.partial(kernel, Z, Q, experts),
        out_shape=jax.ShapeDtypeStruct((T, L), bf16),
        in_specs=[
            pl.BlockSpec(memory_space=pltpu.VMEM),
            pl.BlockSpec(memory_space=pl.ANY),
            pl.BlockSpec(memory_space=pl.ANY),
        ],
        out_specs=pl.BlockSpec(memory_space=pltpu.VMEM),
        scratch_shapes=[
            pltpu.VMEM((Z, CORES, Q, T, L + G), bf16),
            pltpu.VMEM(w_up.shape, bf16),
            pltpu.VMEM(w_down.shape, bf16),
            pltpu.VMEM((Z, Q * T, L), bf16),
            pltpu.VMEM((Z, Q * T, L), bf16),
            pltpu.VMEM((Z, Q, T, L), bf16),
            pltpu.VMEM((Z if Q > 1 else 1, 2, T // 2, L), bf16),
            pltpu.VMEM((Z if Q > 1 else 1, 2, T, L), bf16),
            pltpu.VMEM((Z, T, L), bf16),
            pltpu.VMEM((Z, T, L), bf16),
            pltpu.VMEM((T, L), jnp.float32),
            pltpu.VMEM((G, local_experts * 128), bf16),
            pltpu.SemaphoreType.DMA((Z, 9)),
            pltpu.SemaphoreType.DMA((Z, 9)),
            pltpu.SemaphoreType.DMA((Z, 6)),
            pltpu.SemaphoreType.DMA((Z, 6)),
            pltpu.SemaphoreType.DMA((3,)),
        ],
        compiler_params=pltpu.CompilerParams(
            collective_id=0, has_side_effects=True, vmem_limit_bytes=64 * 1024 * 1024 - 65536
        ),
    )(rows, w_up, w_down)


def solution(mesh):
    in_specs = (
        P(("groups", "row"), None),
        P(("groups", "row"), None),
        P(("groups", "row"), None),
        P("row", None, None),
        P("row", None, None),
    )
    out_specs = P(("groups", "row"), None)
    return jax.shard_map(
        functools.partial(body, mesh.shape["groups"]),
        mesh=mesh, in_specs=in_specs, out_specs=out_specs, check_vma=False,
    )
```

```python
import functools
import jax
import jax.numpy as jnp
from jax import lax
from jax.experimental import pallas as pl
from jax.experimental.pallas import tpu as pltpu
from jax.sharding import PartitionSpec as P

CORES = 2


def kernel(Z, Q, experts, xin, wu_hbm, wd_hbm, out, X, wu, wd, PP, RP, R, DH, XY, S, ZR, F, sel, sa, ra, sr, rr, wsem):
    T, W = xin.shape
    local_experts, H, L = wu.shape
    G = W - L
    half = T // 2
    layer = CORES * Q
    me = lax.axis_index("row")
    c = lax.rem(me, CORES)
    q = lax.rem(me // CORES, Q)
    z = me // layer
    inner = lax.rem(me, layer)
    partner = me + 1 - 2 * c
    if Q > 1:
        x = lax.rem(q, 2)
        y = q // 2
        xn, yn = me + CORES * (1 - 2 * x), me + 2 * CORES * (1 - 2 * y)
        qx, qy, qd = q + 1 - 2 * x, q + 2 * (1 - 2 * y), 3 - q

    def remote(src, dst, ssem, rsem, dev):
        return pltpu.make_async_remote_copy(
            src_ref=src, dst_ref=dst, send_sem=ssem, recv_sem=rsem,
            device_id={"row": dev}, device_id_type=pl.DeviceIdType.MESH,
        )

    weights = [
        pltpu.make_async_copy(wu_hbm, wu, wsem.at[0]),
        pltpu.make_async_copy(wd_hbm, wd, wsem.at[1]),
    ]
    local = pltpu.make_async_copy(xin, X.at[0, c, q], wsem.at[2])
    local.start()
    for w in weights:
        w.start()

    barrier = pltpu.get_barrier_semaphore()
    near = [partner] + ([xn, yn] if Q > 1 else [])
    for dev in near:
        pl.semaphore_signal(barrier, inc=1, device_id={"row": dev}, device_id_type=pl.DeviceIdType.MESH)

    def below(k):
        return lax.rem(z - k + Z, Z) * layer + inner

    def above(k):
        return lax.rem(z + k, Z) * layer + inner

    def greet(k, carry):
        pl.semaphore_signal(barrier, inc=1, device_id={"row": below(k)}, device_id_type=pl.DeviceIdType.MESH)
        return carry

    lax.fori_loop(1, Z, greet, 0)
    pl.semaphore_wait(barrier, len(near) + Z - 1)

    def zcopy(k):
        return remote(xin, X.at[k, c, q], sa.at[k, 0], ra.at[k, 0], below(k))

    def xcopy(k):
        return remote(X.at[k, c, q], X.at[k, c, q], sa.at[k, 1], ra.at[k, 1], xn)

    def ycopy(k):
        return remote(X.at[k, c, q], X.at[k, c, q], sa.at[k, 2], ra.at[k, 2], yn)

    def top(k, slot):
        ref = X.at[k, c, slot, pl.ds(0, half)]
        return remote(ref, ref, sa.at[k, 3], ra.at[k, 3], yn)

    def bottom(k, slot):
        ref = X.at[k, c, slot, pl.ds(half, half)]
        return remote(ref, ref, sa.at[k, 4], ra.at[k, 4], xn)

    def across(k, slot, i, plane):
        ref = X.at[k, plane, slot]
        return remote(ref, ref, sa.at[k, 5 + i], ra.at[k, 5 + i], partner)

    def arrived(k, ref, i):
        remote(ref, ref, sa.at[k, i], ra.at[k, i], partner).wait_recv()

    def ag_send(k):
        if Q > 1:
            xcopy(k).start()
            ycopy(k).start()
        across(k, q, 0, c).start()

    def ag_relay(k):
        if Q > 1:
            arrived(k, X.at[k, c, qx], 1)
            top(k, qx).start()
            arrived(k, X.at[k, c, qy], 2)
            bottom(k, qy).start()
            across(k, qx, 1, c).start()
            across(k, qy, 2, c).start()

    def ag_last(k):
        if Q > 1:
            arrived(k, X.at[k, c, qd, pl.ds(0, half)], 3)
            arrived(k, X.at[k, c, qd, pl.ds(half, half)], 4)
            across(k, qd, 3, c).start()

    def ag_other(k):
        arrived(k, X.at[k, 1 - c, q], 5)
        if Q > 1:
            arrived(k, X.at[k, 1 - c, qx], 6)
            arrived(k, X.at[k, 1 - c, qy], 7)
            arrived(k, X.at[k, 1 - c, qd], 8)

    def compute(k, plane):
        rows = X[k, plane, :, :, pl.ds(0, L)].reshape(Q * T, L)
        codes = X[k, plane, :, :, pl.ds(L, G)].reshape(Q * T, G)
        weight = jnp.dot(codes, sel[...], preferred_element_type=jnp.float32)
        total = None
        for e in range(local_experts):
            hidden = lax.dot_general(rows, wu[e], (((1,), (1,)), ((), ())), preferred_element_type=jnp.float32)
            active = jnp.square(jnp.maximum(hidden, 0.0)).astype(jnp.bfloat16)
            part = jnp.dot(active, wd[e], preferred_element_type=jnp.float32)
            part = part * jnp.tile(weight[:, e * 128 : (e + 1) * 128], (1, L // 128))
            total = part if total is None else total + part
        return total

    def swap(k):
        return remote(PP.at[k], RP.at[k], sr.at[k, 0], rr.at[k, 0], partner)

    def dtop(k):
        return remote(R.at[k, qd, pl.ds(0, half)], DH.at[k, 0], sr.at[k, 1], rr.at[k, 1], yn)

    def dbottom(k):
        return remote(R.at[k, qd, pl.ds(half, half)], DH.at[k, 1], sr.at[k, 2], rr.at[k, 2], xn)

    def xsum(k):
        return remote(R.at[k, qx], XY.at[k, 0], sr.at[k, 3], rr.at[k, 3], xn)

    def ysum(k):
        return remote(R.at[k, qy], XY.at[k, 1], sr.at[k, 4], rr.at[k, 4], yn)

    def zsum(k):
        return remote(S.at[k], ZR.at[k], sr.at[k, 5], rr.at[k, 5], above(k))

    def rs_near(k):
        if Q > 1:
            dtop(k).wait_recv()
            R[k, qx, pl.ds(0, half)] = (
                R[k, qx, pl.ds(0, half)].astype(jnp.float32) + DH[k, 0].astype(jnp.float32)
            ).astype(jnp.bfloat16)
            xsum(k).start()
            dbottom(k).wait_recv()
            R[k, qy, pl.ds(half, half)] = (
                R[k, qy, pl.ds(half, half)].astype(jnp.float32) + DH[k, 1].astype(jnp.float32)
            ).astype(jnp.bfloat16)
            ysum(k).start()

    def rs_far(k):
        value = R[k, q].astype(jnp.float32)
        if Q > 1:
            xsum(k).wait_recv()
            value = value + XY[k, 0].astype(jnp.float32)
            ysum(k).wait_recv()
            value = value + XY[k, 1].astype(jnp.float32)

        @pl.when(k == 0)
        def _():
            F[...] = value

        @pl.when(k > 0)
        def _():
            S[k] = value.astype(jnp.bfloat16)
            zsum(k).start()

    local.wait()
    ag_send(0)

    def send_down(k, carry):
        zcopy(k).start()
        return carry

    lax.fori_loop(1, Z, send_down, 0)
    entry = lax.rem(lax.broadcasted_iota(jnp.int32, sel.shape, 0), experts)
    lane = lax.broadcasted_iota(jnp.int32, sel.shape, 1) // 128
    used = lax.broadcasted_iota(jnp.int32, sel.shape, 0) < 2 * experts
    sel[...] = jnp.where((entry == me * local_experts + lane) & used, 1.0, 0.0).astype(jnp.bfloat16)
    ag_relay(0)
    ag_last(0)
    for w in weights:
        w.wait()

    def step(k, carry):
        ag_other(k)

        @pl.when(k + 1 < Z)
        def _():
            arrived(k + 1, X.at[k + 1, c, q], 0)
            ag_send(k + 1)

        PP[k] = compute(k, 1 - c).astype(jnp.bfloat16)
        swap(k).start()

        @pl.when(k > 0)
        def _():
            rs_near(k - 1)

        @pl.when(k + 1 < Z)
        def _():
            ag_relay(k + 1)

        mine = compute(k, c)
        swap(k).wait_recv()
        R[k] = (mine + RP[k].astype(jnp.float32)).astype(jnp.bfloat16).reshape(Q, T, L)
        if Q > 1:
            dtop(k).start()
            dbottom(k).start()

        @pl.when(k + 1 < Z)
        def _():
            ag_last(k + 1)

        @pl.when(k > 0)
        def _():
            rs_far(k - 1)

        return carry

    lax.fori_loop(0, Z, step, 0)
    rs_near(Z - 1)
    rs_far(Z - 1)

    def collect(k, carry):
        zsum(k).wait_recv()
        F[...] += ZR[k].astype(jnp.float32)
        return carry

    lax.fori_loop(1, Z, collect, 0)
    out[...] = F[...].astype(out.dtype)

    def drain(k, carry):
        across(k, q, 0, c).wait_send()
        swap(k).wait_send()
        if Q > 1:
            xcopy(k).wait_send()
            ycopy(k).wait_send()
            top(k, qx).wait_send()
            bottom(k, qy).wait_send()
            across(k, qx, 1, c).wait_send()
            across(k, qy, 2, c).wait_send()
            across(k, qd, 3, c).wait_send()
            dtop(k).wait_send()
            dbottom(k).wait_send()
            xsum(k).wait_send()
            ysum(k).wait_send()

        @pl.when(k > 0)
        def _():
            zcopy(k).wait_send()
            zsum(k).wait_send()

        return carry

    lax.fori_loop(0, Z, drain, 0)


def body(groups, latents, expert_ids, gates, w_up, w_down):
    n = lax.axis_size("row")
    T, L = latents.shape
    local_experts, unused, H = w_up.shape
    experts = n * local_experts
    Q = 4 if groups == 1 and n % (4 * CORES) == 0 else 1
    Z = n // (CORES * Q)
    labels = jnp.arange(experts, dtype=jnp.int32)
    dense = jnp.sum(
        jnp.where(expert_ids[:, :, None] == labels[None, None, :], gates[:, :, None], 0.0), axis=1
    )
    coarse = lax.reduce_precision(dense, 8, 7)
    G = -(-2 * experts // 128) * 128
    pad = jnp.zeros((T, G - 2 * experts), jnp.bfloat16)
    rows = jnp.concatenate(
        [latents, coarse.astype(jnp.bfloat16), (dense - coarse).astype(jnp.bfloat16), pad], axis=1
    )
    bf16 = jnp.bfloat16
    return pl.pallas_call(
        functools.partial(kernel, Z, Q, experts),
        out_shape=jax.ShapeDtypeStruct((T, L), bf16),
        in_specs=[
            pl.BlockSpec(memory_space=pltpu.VMEM),
            pl.BlockSpec(memory_space=pl.ANY),
            pl.BlockSpec(memory_space=pl.ANY),
        ],
        out_specs=pl.BlockSpec(memory_space=pltpu.VMEM),
        scratch_shapes=[
            pltpu.VMEM((Z, CORES, Q, T, L + G), bf16),
            pltpu.VMEM(w_down.shape, bf16),
            pltpu.VMEM(w_down.shape, bf16),
            pltpu.VMEM((Z, Q * T, L), bf16),
            pltpu.VMEM((Z, Q * T, L), bf16),
            pltpu.VMEM((Z, Q, T, L), bf16),
            pltpu.VMEM((Z if Q > 1 else 1, 2, T // 2, L), bf16),
            pltpu.VMEM((Z if Q > 1 else 1, 2, T, L), bf16),
            pltpu.VMEM((Z, T, L), bf16),
            pltpu.VMEM((Z, T, L), bf16),
            pltpu.VMEM((T, L), jnp.float32),
            pltpu.VMEM((G, local_experts * 128), bf16),
            pltpu.SemaphoreType.DMA((Z, 9)),
            pltpu.SemaphoreType.DMA((Z, 9)),
            pltpu.SemaphoreType.DMA((Z, 6)),
            pltpu.SemaphoreType.DMA((Z, 6)),
            pltpu.SemaphoreType.DMA((3,)),
        ],
        compiler_params=pltpu.CompilerParams(
            collective_id=0, has_side_effects=True, vmem_limit_bytes=64 * 1024 * 1024 - 65536
        ),
    )(rows, jnp.swapaxes(w_up,1,2), w_down)


def solution(mesh):
    in_specs = (
        P(("groups", "row"), None),
        P(("groups", "row"), None),
        P(("groups", "row"), None),
        P("row", None, None),
        P("row", None, None),
    )
    out_specs = P(("groups", "row"), None)
    return jax.shard_map(
        functools.partial(body, mesh.shape["groups"]),
        mesh=mesh, in_specs=in_specs, out_specs=out_specs, check_vma=False,
    )
```

```python
import functools
import jax
import jax.numpy as jnp
from jax import lax
from jax.experimental import pallas as pl
from jax.experimental.pallas import tpu as pltpu
from jax.sharding import PartitionSpec as P

CORES = 2


def kernel(Z, Q, experts, xin, wu_hbm, wd_hbm, out, X, wu, wd, PP, RP, R, DH, XY, S, ZR, F, sel, sa, ra, sr, rr, wsem):
    T, W = xin.shape
    local_experts, H, L = wu.shape
    G = W - L
    half = T // 2
    layer = CORES * Q
    me = lax.axis_index("row")
    c = lax.rem(me, CORES)
    q = lax.rem(me // CORES, Q)
    z = me // layer
    inner = lax.rem(me, layer)
    partner = me + 1 - 2 * c
    if Q > 1:
        x = lax.rem(q, 2)
        y = q // 2
        xn, yn = me + CORES * (1 - 2 * x), me + 2 * CORES * (1 - 2 * y)
        qx, qy, qd = q + 1 - 2 * x, q + 2 * (1 - 2 * y), 3 - q

    def remote(src, dst, ssem, rsem, dev):
        return pltpu.make_async_remote_copy(
            src_ref=src, dst_ref=dst, send_sem=ssem, recv_sem=rsem,
            device_id={"row": dev}, device_id_type=pl.DeviceIdType.MESH,
        )

    weights = [
        pltpu.make_async_copy(wu_hbm, wu, wsem.at[0]),
        pltpu.make_async_copy(wd_hbm, wd, wsem.at[1]),
    ]
    local = pltpu.make_async_copy(xin, X.at[0, c, q], wsem.at[2])
    local.start()
    for w in weights:
        w.start()

    barrier = pltpu.get_barrier_semaphore()
    near = [partner] + ([xn, yn] if Q > 1 else [])
    for dev in near:
        pl.semaphore_signal(barrier, inc=1, device_id={"row": dev}, device_id_type=pl.DeviceIdType.MESH)

    def below(k):
        return lax.rem(z - k + Z, Z) * layer + inner

    def above(k):
        return lax.rem(z + k, Z) * layer + inner

    def greet(k, carry):
        pl.semaphore_signal(barrier, inc=1, device_id={"row": below(k)}, device_id_type=pl.DeviceIdType.MESH)
        return carry

    lax.fori_loop(1, Z, greet, 0)
    pl.semaphore_wait(barrier, len(near) + Z - 1)

    def zcopy(k):
        return remote(xin, X.at[k, c, q], sa.at[k, 0], ra.at[k, 0], below(k))

    def xcopy(k):
        return remote(X.at[k, c, q], X.at[k, c, q], sa.at[k, 1], ra.at[k, 1], xn)

    def ycopy(k):
        return remote(X.at[k, c, q], X.at[k, c, q], sa.at[k, 2], ra.at[k, 2], yn)

    def top(k, slot):
        ref = X.at[k, c, slot, pl.ds(0, half)]
        return remote(ref, ref, sa.at[k, 3], ra.at[k, 3], yn)

    def bottom(k, slot):
        ref = X.at[k, c, slot, pl.ds(half, half)]
        return remote(ref, ref, sa.at[k, 4], ra.at[k, 4], xn)

    def across(k, slot, i, plane):
        ref = X.at[k, plane, slot]
        return remote(ref, ref, sa.at[k, 5 + i], ra.at[k, 5 + i], partner)

    def arrived(k, ref, i):
        remote(ref, ref, sa.at[k, i], ra.at[k, i], partner).wait_recv()

    def ag_send(k):
        if Q > 1:
            xcopy(k).start()
            ycopy(k).start()
        across(k, q, 0, c).start()

    def ag_relay(k):
        if Q > 1:
            arrived(k, X.at[k, c, qx], 1)
            top(k, qx).start()
            arrived(k, X.at[k, c, qy], 2)
            bottom(k, qy).start()
            across(k, qx, 1, c).start()
            across(k, qy, 2, c).start()

    def ag_last(k):
        if Q > 1:
            arrived(k, X.at[k, c, qd, pl.ds(0, half)], 3)
            arrived(k, X.at[k, c, qd, pl.ds(half, half)], 4)
            across(k, qd, 3, c).start()

    def ag_other(k):
        arrived(k, X.at[k, 1 - c, q], 5)
        if Q > 1:
            arrived(k, X.at[k, 1 - c, qx], 6)
            arrived(k, X.at[k, 1 - c, qy], 7)
            arrived(k, X.at[k, 1 - c, qd], 8)

    def compute(k, plane):
        rows = X[k, plane, :, :, pl.ds(0, L)].reshape(Q * T, L)
        codes = X[k, plane, :, :, pl.ds(L, G)].reshape(Q * T, G)
        weight = jnp.dot(codes, sel[...], preferred_element_type=jnp.float32)
        total = None
        for e in range(local_experts):
            hidden = lax.dot_general(rows, wu[e], (((1,), (1,)), ((), ())), preferred_element_type=jnp.float32)
            active = jnp.square(jnp.maximum(hidden, 0.0)).astype(jnp.bfloat16)
            part = jnp.dot(active, wd[e], preferred_element_type=jnp.float32)
            part = part * jnp.tile(weight[:, e * 128 : (e + 1) * 128], (1, L // 128))
            total = part if total is None else total + part
        return total

    def swap(k):
        return remote(PP.at[k], RP.at[k], sr.at[k, 0], rr.at[k, 0], partner)

    def dtop(k):
        return remote(R.at[k, qd, pl.ds(0, half)], DH.at[k, 0], sr.at[k, 1], rr.at[k, 1], yn)

    def dbottom(k):
        return remote(R.at[k, qd, pl.ds(half, half)], DH.at[k, 1], sr.at[k, 2], rr.at[k, 2], xn)

    def xsum(k):
        return remote(R.at[k, qx], XY.at[k, 0], sr.at[k, 3], rr.at[k, 3], xn)

    def ysum(k):
        return remote(R.at[k, qy], XY.at[k, 1], sr.at[k, 4], rr.at[k, 4], yn)

    def zsum(k):
        return remote(S.at[k], ZR.at[k], sr.at[k, 5], rr.at[k, 5], above(k))

    def rs_near(k):
        if Q > 1:
            dtop(k).wait_recv()
            R[k, qx, pl.ds(0, half)] = (
                R[k, qx, pl.ds(0, half)].astype(jnp.float32) + DH[k, 0].astype(jnp.float32)
            ).astype(jnp.bfloat16)
            xsum(k).start()
            dbottom(k).wait_recv()
            R[k, qy, pl.ds(half, half)] = (
                R[k, qy, pl.ds(half, half)].astype(jnp.float32) + DH[k, 1].astype(jnp.float32)
            ).astype(jnp.bfloat16)
            ysum(k).start()

    def rs_far(k):
        value = R[k, q].astype(jnp.float32)
        if Q > 1:
            xsum(k).wait_recv()
            value = value + XY[k, 0].astype(jnp.float32)
            ysum(k).wait_recv()
            value = value + XY[k, 1].astype(jnp.float32)

        @pl.when(k == 0)
        def _():
            F[...] = value

        @pl.when(k > 0)
        def _():
            S[k] = value.astype(jnp.bfloat16)
            zsum(k).start()

    if Z > 1:
        zcopy(1).start()
    local.wait()
    ag_send(0)
    entry = lax.rem(lax.broadcasted_iota(jnp.int32, sel.shape, 0), experts)
    lane = lax.broadcasted_iota(jnp.int32, sel.shape, 1) // 128
    used = lax.broadcasted_iota(jnp.int32, sel.shape, 0) < 2 * experts
    sel[...] = jnp.where((entry == me * local_experts + lane) & used, 1.0, 0.0).astype(jnp.bfloat16)
    ag_relay(0)
    if Z > 2:
        zcopy(2).start()
    if Z > 1:
        arrived(1, X.at[1, c, q], 0)
        ag_send(1)
    ag_last(0)
    for w in weights:
        w.wait()

    def step(k, carry):
        ag_other(k)
        PP[k] = compute(k, 1 - c).astype(jnp.bfloat16)
        swap(k).start()

        @pl.when(k + 1 < Z)
        def _():
            ag_relay(k + 1)

        @pl.when(k > 0)
        def _():
            rs_near(k - 1)

        @pl.when(k + 2 < Z)
        def _():
            arrived(k + 2, X.at[k + 2, c, q], 0)
            ag_send(k + 2)

        @pl.when(k + 3 < Z)
        def _():
            zcopy(k + 3).start()

        @pl.when(k > 1)
        def _():
            rs_far(k - 2)

        mine = compute(k, c)
        swap(k).wait_recv()
        R[k] = (mine + RP[k].astype(jnp.float32)).astype(jnp.bfloat16).reshape(Q, T, L)
        if Q > 1:
            dtop(k).start()
            dbottom(k).start()

        @pl.when(k + 1 < Z)
        def _():
            ag_last(k + 1)

        return carry

    lax.fori_loop(0, Z, step, 0)
    if Z > 1:
        rs_far(Z - 2)
    rs_near(Z - 1)
    rs_far(Z - 1)

    def collect(k, carry):
        zsum(k).wait_recv()
        F[...] += ZR[k].astype(jnp.float32)
        return carry

    lax.fori_loop(1, Z, collect, 0)
    out[...] = F[...].astype(out.dtype)

    def drain(k, carry):
        across(k, q, 0, c).wait_send()
        swap(k).wait_send()
        if Q > 1:
            xcopy(k).wait_send()
            ycopy(k).wait_send()
            top(k, qx).wait_send()
            bottom(k, qy).wait_send()
            across(k, qx, 1, c).wait_send()
            across(k, qy, 2, c).wait_send()
            across(k, qd, 3, c).wait_send()
            dtop(k).wait_send()
            dbottom(k).wait_send()
            xsum(k).wait_send()
            ysum(k).wait_send()

        @pl.when(k > 0)
        def _():
            zcopy(k).wait_send()
            zsum(k).wait_send()

        return carry

    lax.fori_loop(0, Z, drain, 0)


def body(groups, latents, expert_ids, gates, w_up, w_down):
    n = lax.axis_size("row")
    T, L = latents.shape
    local_experts, unused, H = w_up.shape
    experts = n * local_experts
    Q = 4 if groups == 1 and n % (4 * CORES) == 0 else 1
    Z = n // (CORES * Q)
    labels = jnp.arange(experts, dtype=jnp.int32)
    dense = jnp.sum(
        jnp.where(expert_ids[:, :, None] == labels[None, None, :], gates[:, :, None], 0.0), axis=1
    )
    coarse = lax.reduce_precision(dense, 8, 7)
    G = -(-2 * experts // 128) * 128
    pad = jnp.zeros((T, G - 2 * experts), jnp.bfloat16)
    rows = jnp.concatenate(
        [latents, coarse.astype(jnp.bfloat16), (dense - coarse).astype(jnp.bfloat16), pad], axis=1
    )
    bf16 = jnp.bfloat16
    return pl.pallas_call(
        functools.partial(kernel, Z, Q, experts),
        out_shape=jax.ShapeDtypeStruct((T, L), bf16),
        in_specs=[
            pl.BlockSpec(memory_space=pltpu.VMEM),
            pl.BlockSpec(memory_space=pl.ANY),
            pl.BlockSpec(memory_space=pl.ANY),
        ],
        out_specs=pl.BlockSpec(memory_space=pltpu.VMEM),
        scratch_shapes=[
            pltpu.VMEM((Z, CORES, Q, T, L + G), bf16),
            pltpu.VMEM(w_down.shape, bf16),
            pltpu.VMEM(w_down.shape, bf16),
            pltpu.VMEM((Z, Q * T, L), bf16),
            pltpu.VMEM((Z, Q * T, L), bf16),
            pltpu.VMEM((Z, Q, T, L), bf16),
            pltpu.VMEM((Z if Q > 1 else 1, 2, T // 2, L), bf16),
            pltpu.VMEM((Z if Q > 1 else 1, 2, T, L), bf16),
            pltpu.VMEM((Z, T, L), bf16),
            pltpu.VMEM((Z, T, L), bf16),
            pltpu.VMEM((T, L), jnp.float32),
            pltpu.VMEM((G, local_experts * 128), bf16),
            pltpu.SemaphoreType.DMA((Z, 9)),
            pltpu.SemaphoreType.DMA((Z, 9)),
            pltpu.SemaphoreType.DMA((Z, 6)),
            pltpu.SemaphoreType.DMA((Z, 6)),
            pltpu.SemaphoreType.DMA((3,)),
        ],
        compiler_params=pltpu.CompilerParams(
            collective_id=0, has_side_effects=True, vmem_limit_bytes=64 * 1024 * 1024 - 65536
        ),
    )(rows, jnp.swapaxes(w_up,1,2), w_down)


def solution(mesh):
    in_specs = (
        P(("groups", "row"), None),
        P(("groups", "row"), None),
        P(("groups", "row"), None),
        P("row", None, None),
        P("row", None, None),
    )
    out_specs = P(("groups", "row"), None)
    return jax.shard_map(
        functools.partial(body, mesh.shape["groups"]),
        mesh=mesh, in_specs=in_specs, out_specs=out_specs, check_vma=False,
    )
```

```python
import functools
import jax
import jax.numpy as jnp
from jax import lax
from jax.experimental import pallas as pl
from jax.experimental.pallas import tpu as pltpu
from jax.sharding import PartitionSpec as P

CORES = 2


def kernel(Z, Q, experts, xin, wu_hbm, wd_hbm, out, X, wu, wd, PP, RP, R, DH, XY, S, ZR, F, sel, sa, ra, sr, rr, wsem):
    T, W = xin.shape
    local_experts, H, L = wu.shape
    G = W - L
    half = T // 2
    layer = CORES * Q
    me = lax.axis_index("row")
    c = lax.rem(me, CORES)
    q = lax.rem(me // CORES, Q)
    z = me // layer
    inner = lax.rem(me, layer)
    partner = me + 1 - 2 * c
    if Q > 1:
        x = lax.rem(q, 2)
        y = q // 2
        xn, yn = me + CORES * (1 - 2 * x), me + 2 * CORES * (1 - 2 * y)
        qx, qy, qd = q + 1 - 2 * x, q + 2 * (1 - 2 * y), 3 - q

    def remote(src, dst, ssem, rsem, dev):
        return pltpu.make_async_remote_copy(
            src_ref=src, dst_ref=dst, send_sem=ssem, recv_sem=rsem,
            device_id={"row": dev}, device_id_type=pl.DeviceIdType.MESH,
        )

    weights = [
        pltpu.make_async_copy(wu_hbm, wu, wsem.at[0]),
        pltpu.make_async_copy(wd_hbm, wd, wsem.at[1]),
    ]
    local = pltpu.make_async_copy(xin, X.at[0, c, q], wsem.at[2])
    local.start()
    for w in weights:
        w.start()

    barrier = pltpu.get_barrier_semaphore()
    near = [partner] + ([xn, yn] if Q > 1 else [])
    for dev in near:
        pl.semaphore_signal(barrier, inc=1, device_id={"row": dev}, device_id_type=pl.DeviceIdType.MESH)

    def below(k):
        return lax.rem(z - k + Z, Z) * layer + inner

    def above(k):
        return lax.rem(z + k, Z) * layer + inner

    def greet(k, carry):
        pl.semaphore_signal(barrier, inc=1, device_id={"row": below(k)}, device_id_type=pl.DeviceIdType.MESH)
        return carry

    lax.fori_loop(1, Z, greet, 0)
    pl.semaphore_wait(barrier, len(near) + Z - 1)

    def zcopy(k):
        return remote(xin, X.at[k, c, q], sa.at[k, 0], ra.at[k, 0], below(k))

    def xcopy(k):
        return remote(X.at[k, c, q], X.at[k, c, q], sa.at[k, 1], ra.at[k, 1], xn)

    def ycopy(k):
        return remote(X.at[k, c, q], X.at[k, c, q], sa.at[k, 2], ra.at[k, 2], yn)

    def top(k, slot):
        ref = X.at[k, c, slot, pl.ds(0, half)]
        return remote(ref, ref, sa.at[k, 3], ra.at[k, 3], yn)

    def bottom(k, slot):
        ref = X.at[k, c, slot, pl.ds(half, half)]
        return remote(ref, ref, sa.at[k, 4], ra.at[k, 4], xn)

    def across(k, slot, i, plane):
        ref = X.at[k, plane, slot]
        return remote(ref, ref, sa.at[k, 5 + i], ra.at[k, 5 + i], partner)

    def arrived(k, ref, i):
        remote(ref, ref, sa.at[k, i], ra.at[k, i], partner).wait_recv()

    def ag_send(k):
        if Q > 1:
            xcopy(k).start()
            ycopy(k).start()
        across(k, q, 0, c).start()

    def ag_relay(k):
        if Q > 1:
            arrived(k, X.at[k, c, qx], 1)
            top(k, qx).start()
            arrived(k, X.at[k, c, qy], 2)
            bottom(k, qy).start()
            across(k, qx, 1, c).start()
            across(k, qy, 2, c).start()

    def ag_last(k):
        if Q > 1:
            arrived(k, X.at[k, c, qd, pl.ds(0, half)], 3)
            arrived(k, X.at[k, c, qd, pl.ds(half, half)], 4)
            across(k, qd, 3, c).start()

    def ag_other(k):
        arrived(k, X.at[k, 1 - c, q], 5)
        if Q > 1:
            arrived(k, X.at[k, 1 - c, qx], 6)
            arrived(k, X.at[k, 1 - c, qy], 7)
            arrived(k, X.at[k, 1 - c, qd], 8)

    def compute(k, plane):
        rows = X[k, plane, :, :, pl.ds(0, L)].reshape(Q * T, L)
        codes = X[k, plane, :, :, pl.ds(L, G)].reshape(Q * T, G)
        weight = jnp.dot(codes, sel[...], preferred_element_type=jnp.float32)
        total = None
        for e in range(local_experts):
            hidden = lax.dot_general(rows, wu[e], (((1,), (1,)), ((), ())), preferred_element_type=jnp.float32)
            active = jnp.square(jnp.maximum(hidden, 0.0)).astype(jnp.bfloat16)
            part = jnp.dot(active, wd[e], preferred_element_type=jnp.float32)
            part = part * jnp.tile(weight[:, e * 128 : (e + 1) * 128], (1, L // 128))
            total = part if total is None else total + part
        return total

    def swap(k):
        return remote(PP.at[k], RP.at[k], sr.at[k, 0], rr.at[k, 0], partner)

    def dtop(k):
        return remote(R.at[k, qd, pl.ds(0, half)], DH.at[k, 0], sr.at[k, 1], rr.at[k, 1], yn)

    def dbottom(k):
        return remote(R.at[k, qd, pl.ds(half, half)], DH.at[k, 1], sr.at[k, 2], rr.at[k, 2], xn)

    def xsum(k):
        return remote(R.at[k, qx], XY.at[k, 0], sr.at[k, 3], rr.at[k, 3], xn)

    def ysum(k):
        return remote(R.at[k, qy], XY.at[k, 1], sr.at[k, 4], rr.at[k, 4], yn)

    def zsum(k):
        return remote(S.at[k], ZR.at[k], sr.at[k, 5], rr.at[k, 5], above(k))

    def rs_near(k):
        if Q > 1:
            dtop(k).wait_recv()
            R[k, qx, pl.ds(0, half)] = (
                R[k, qx, pl.ds(0, half)].astype(jnp.float32) + DH[k, 0].astype(jnp.float32)
            ).astype(jnp.bfloat16)
            xsum(k).start()
            dbottom(k).wait_recv()
            R[k, qy, pl.ds(half, half)] = (
                R[k, qy, pl.ds(half, half)].astype(jnp.float32) + DH[k, 1].astype(jnp.float32)
            ).astype(jnp.bfloat16)
            ysum(k).start()

    def rs_far(k):
        value = R[k, q].astype(jnp.float32)
        if Q > 1:
            xsum(k).wait_recv()
            value = value + XY[k, 0].astype(jnp.float32)
            ysum(k).wait_recv()
            value = value + XY[k, 1].astype(jnp.float32)

        @pl.when(k == 0)
        def _():
            F[...] = value

        @pl.when(k > 0)
        def _():
            S[k] = value.astype(jnp.bfloat16)
            zsum(k).start()

    if Z > 1:
        zcopy(1).start()
    local.wait()
    ag_send(0)
    if Z > 2:
        zcopy(2).start()
    entry = lax.rem(lax.broadcasted_iota(jnp.int32, sel.shape, 0), experts)
    lane = lax.broadcasted_iota(jnp.int32, sel.shape, 1) // 128
    used = lax.broadcasted_iota(jnp.int32, sel.shape, 0) < 2 * experts
    sel[...] = jnp.where((entry == me * local_experts + lane) & used, 1.0, 0.0).astype(jnp.bfloat16)
    ag_relay(0)
    if Z > 3:
        zcopy(3).start()
    ag_last(0)
    if Z > 1:
        arrived(1, X.at[1, c, q], 0)
        ag_send(1)
    for w in weights:
        w.wait()

    def step(k, carry):
        ag_other(k)
        PP[k] = compute(k, 1 - c).astype(jnp.bfloat16)
        swap(k).start()

        @pl.when(k + 1 < Z)
        def _():
            ag_relay(k + 1)

        @pl.when(k > 0)
        def _():
            rs_near(k - 1)

        @pl.when(k + 2 < Z)
        def _():
            arrived(k + 2, X.at[k + 2, c, q], 0)
            ag_send(k + 2)

        @pl.when(k + 4 < Z)
        def _():
            zcopy(k + 4).start()

        @pl.when(k > 1)
        def _():
            rs_far(k - 2)

        mine = compute(k, c)
        swap(k).wait_recv()
        R[k] = (mine + RP[k].astype(jnp.float32)).astype(jnp.bfloat16).reshape(Q, T, L)
        if Q > 1:
            dtop(k).start()
            dbottom(k).start()

        @pl.when(k + 1 < Z)
        def _():
            ag_last(k + 1)

        return carry

    lax.fori_loop(0, Z, step, 0)
    if Z > 1:
        rs_far(Z - 2)
    rs_near(Z - 1)
    rs_far(Z - 1)

    def collect(k, carry):
        zsum(k).wait_recv()
        F[...] += ZR[k].astype(jnp.float32)
        return carry

    lax.fori_loop(1, Z, collect, 0)
    out[...] = F[...].astype(out.dtype)

    def drain(k, carry):
        across(k, q, 0, c).wait_send()
        swap(k).wait_send()
        if Q > 1:
            xcopy(k).wait_send()
            ycopy(k).wait_send()
            top(k, qx).wait_send()
            bottom(k, qy).wait_send()
            across(k, qx, 1, c).wait_send()
            across(k, qy, 2, c).wait_send()
            across(k, qd, 3, c).wait_send()
            dtop(k).wait_send()
            dbottom(k).wait_send()
            xsum(k).wait_send()
            ysum(k).wait_send()

        @pl.when(k > 0)
        def _():
            zcopy(k).wait_send()
            zsum(k).wait_send()

        return carry

    lax.fori_loop(0, Z, drain, 0)


def body(groups, latents, expert_ids, gates, w_up, w_down):
    n = lax.axis_size("row")
    T, L = latents.shape
    local_experts, unused, H = w_up.shape
    experts = n * local_experts
    Q = 4 if groups == 1 and n % (4 * CORES) == 0 else 1
    Z = n // (CORES * Q)
    labels = jnp.arange(experts, dtype=jnp.int32)
    dense = jnp.sum(
        jnp.where(expert_ids[:, :, None] == labels[None, None, :], gates[:, :, None], 0.0), axis=1
    )
    coarse = lax.reduce_precision(dense, 8, 7)
    G = -(-2 * experts // 128) * 128
    pad = jnp.zeros((T, G - 2 * experts), jnp.bfloat16)
    rows = jnp.concatenate(
        [latents, coarse.astype(jnp.bfloat16), (dense - coarse).astype(jnp.bfloat16), pad], axis=1
    )
    bf16 = jnp.bfloat16
    return pl.pallas_call(
        functools.partial(kernel, Z, Q, experts),
        out_shape=jax.ShapeDtypeStruct((T, L), bf16),
        in_specs=[
            pl.BlockSpec(memory_space=pltpu.VMEM),
            pl.BlockSpec(memory_space=pl.ANY),
            pl.BlockSpec(memory_space=pl.ANY),
        ],
        out_specs=pl.BlockSpec(memory_space=pltpu.VMEM),
        scratch_shapes=[
            pltpu.VMEM((Z, CORES, Q, T, L + G), bf16),
            pltpu.VMEM(w_down.shape, bf16),
            pltpu.VMEM(w_down.shape, bf16),
            pltpu.VMEM((Z, Q * T, L), bf16),
            pltpu.VMEM((Z, Q * T, L), bf16),
            pltpu.VMEM((Z, Q, T, L), bf16),
            pltpu.VMEM((Z if Q > 1 else 1, 2, T // 2, L), bf16),
            pltpu.VMEM((Z if Q > 1 else 1, 2, T, L), bf16),
            pltpu.VMEM((Z, T, L), bf16),
            pltpu.VMEM((Z, T, L), bf16),
            pltpu.VMEM((T, L), jnp.float32),
            pltpu.VMEM((G, local_experts * 128), bf16),
            pltpu.SemaphoreType.DMA((Z, 9)),
            pltpu.SemaphoreType.DMA((Z, 9)),
            pltpu.SemaphoreType.DMA((Z, 6)),
            pltpu.SemaphoreType.DMA((Z, 6)),
            pltpu.SemaphoreType.DMA((3,)),
        ],
        compiler_params=pltpu.CompilerParams(
            collective_id=0, has_side_effects=True, vmem_limit_bytes=64 * 1024 * 1024 - 65536
        ),
    )(rows, jnp.swapaxes(w_up,1,2), w_down)


def solution(mesh):
    in_specs = (
        P(("groups", "row"), None),
        P(("groups", "row"), None),
        P(("groups", "row"), None),
        P("row", None, None),
        P("row", None, None),
    )
    out_specs = P(("groups", "row"), None)
    return jax.shard_map(
        functools.partial(body, mesh.shape["groups"]),
        mesh=mesh, in_specs=in_specs, out_specs=out_specs, check_vma=False,
    )
```
